32 devices in a mesh: wide: 4 (over y, core), narrow: 8 (over z, x).
Axes of the slice: x: 2, y: 2, z: 4, core: 2. Of those that a mesh axis runs over, the one named last changes fastest.
Arguments:
- transmission: float32 [2, 4096, 2048], P(None, 'narrow', 'wide'), may hold values from -5 to 5
- probe_wave: float32 [2, 256, 256], replicated, may hold values from -5 to 5
- positions: int32 [8, 4, 2, 6, 2], P('narrow', 'wide'), may hold values from 0 to 512, as said below
- counts: int32 [8, 4, 2], P('narrow', 'wide'), may hold values from 1 to 6, as said below
- measured: float32 [8, 4, 2, 6, 256, 256], P('narrow', 'wide'), may hold values from 0 to 2
Outputs:
- updated: float32 [2, 4096, 2048], P(None, 'narrow', 'wide')
The draws below stay inside these ranges and needn't reach their ends.
Inputs may be any that keep to these rules, and one draw needn't show every extreme that they name: `positions`: offsets in pixels from the upper left corner of the tile's reach, which begins 128 pixels before the tile; both ends are taken in every draw. `counts`: some tile and subset has all 6 slots live in every draw; loads differ from tile to tile.
All inputs are finite; a program needn't handle non-finite values.
Results may differ from the reference program's by a relative error of at most 0.0001.
Values sent between devices are 32-bit elements; how exact they have to be, the bound alone decides.
No kernel may reach another device: no remote copies, remote signals or barrier semaphores. Data moves between devices by JAX's collectives and lax.ppermute only.
A program may use at most 128 MiB of HBM per device.

```python
import jax
import jax.numpy as jnp
from jax import lax

TILE = 512
HALO = 128
WIN = 256
SLOTS = 6
NR = 4096
NC = 2048
N_WIDE = 4
N_NARROW = 8


def draw_counts(key, part):
    upper_bound = max(2, 2 * SLOTS // 3 + 1)
    drawn_counts = jax.random.randint(key, (N_NARROW * N_WIDE * 2,), 1, upper_bound, dtype=jnp.int32)
    chosen = jax.random.randint(jax.random.fold_in(key, 7), (), 0, N_NARROW * N_WIDE * 2, dtype=jnp.int32)
    drawn_counts = drawn_counts.at[chosen].set(SLOTS)
    return drawn_counts.reshape(N_NARROW, N_WIDE, 2)


def draw_positions(key, part):
    element_total = N_NARROW * N_WIDE * 2 * SLOTS * 2
    drawn_offsets = jax.random.randint(key, (element_total,), 0, TILE + 1, dtype=jnp.int32)
    chosen = jax.random.randint(jax.random.fold_in(key, 11), (), 0, element_total, dtype=jnp.int32)
    drawn_offsets = drawn_offsets.at[chosen].set(TILE)
    drawn_offsets = drawn_offsets.at[(chosen + 1) % element_total].set(0)
    return drawn_offsets.reshape(N_NARROW, N_WIDE, 2, SLOTS, 2)


def shard_levels(stream_key, shape, shards, least, high):
    loudness = 1.0
    for position, blocks in shards:
        heights = jax.random.uniform(jax.random.fold_in(jax.random.fold_in(stream_key, 6), position), (blocks,), jnp.float32, least / len(shards), high / len(shards))
        loudness = loudness * jnp.repeat(jnp.exp(heights), shape[position] // blocks).reshape((-1,) + (1,) * (len(shape) - 1 - position))
    return loudness


def scatter_about(key, dims, deviation, limit, split=(), kind=jnp.bfloat16):
    array = deviation * jax.random.normal(key, dims, jnp.float32)
    if split:
        array = array * shard_levels(key, dims, split, -0.22, 0.18)
    return jnp.clip(array, -limit, limit).astype(kind)


def setup_inputs(seed: int = 0) -> dict:
    splits = jax.random.split(jax.random.key(seed), 6)
    transmission = scatter_about(splits[0], (2, NR, NC), 0.7, 5.0, ((1, 8), (2, 4)), jnp.float32)
    probe_wave = scatter_about(splits[1], (2, WIN, WIN), 1.0, 5.0, (), jnp.float32)
    positions = draw_positions(jax.random.fold_in(splits[5], 71), 0)
    counts = draw_counts(jax.random.fold_in(splits[5], 71), 0)
    measured = jnp.clip(2.0 * jax.random.uniform(splits[4], (N_NARROW, N_WIDE, 2, SLOTS, WIN, WIN), jnp.float32) ** shard_levels(splits[4], (N_NARROW, N_WIDE, 2, SLOTS, WIN, WIN), ((0, 8), (1, 4)), -0.2, 0.2), 0.0, 2.0)
    return {"transmission": transmission, "probe_wave": probe_wave, "positions": positions, "counts": counts, "measured": measured}


FLOOR_VALUE = 0.5


def project(window_data, probe_re, probe_im, amplitude):
    wave_re = probe_re * window_data[0] - probe_im * window_data[1]
    wave_im = probe_re * window_data[1] + probe_im * window_data[0]
    spectrum = jnp.fft.fft2(lax.complex(wave_re, wave_im), norm="ortho")
    magnitude = jnp.maximum(jnp.abs(spectrum), FLOOR_VALUE)
    projected = spectrum * (amplitude / magnitude)
    returned = jnp.fft.ifft2(projected, norm="ortho")
    diff_re = jnp.real(returned) - wave_re
    diff_im = jnp.imag(returned) - wave_im
    grad_re = probe_re * diff_re + probe_im * diff_im
    grad_im = probe_re * diff_im - probe_im * diff_re
    return jnp.stack([grad_re, grad_im])


def reference(transmission, probe_wave, positions, counts, measured):
    probe_re = probe_wave[0]
    probe_im = probe_wave[1]
    step_scale = 1.0 / jnp.max(probe_re * probe_re + probe_im * probe_im)
    padded = jnp.pad(transmission, ((0, 0), (HALO, HALO), (HALO, HALO)))
    slot_total = N_NARROW * N_WIDE * 2 * SLOTS
    flat_positions = positions.reshape(slot_total, 2).astype(jnp.int32)
    flat_measured = measured.reshape(slot_total, WIN, WIN)
    flat_counts = counts.reshape(N_NARROW * N_WIDE * 2).astype(jnp.int32)

    def accumulate(number, gradient):
        tile_index = number // (2 * SLOTS)
        subset_index = (number // SLOTS) % 2
        slot_index = number % SLOTS
        row_start = ((tile_index // N_WIDE) * TILE + flat_positions[number, 0]).astype(jnp.int32)
        col_start = ((tile_index % N_WIDE) * TILE + flat_positions[number, 1]).astype(jnp.int32)
        zero_start = jnp.zeros((), jnp.int32)
        window_data = lax.dynamic_slice(padded, (zero_start, row_start, col_start), (2, WIN, WIN))
        live_flag = (slot_index < flat_counts[tile_index * 2 + subset_index]).astype(padded.dtype)
        contribution = project(window_data, probe_re, probe_im, flat_measured[number]) * live_flag
        current = lax.dynamic_slice(gradient, (zero_start, row_start, col_start), (2, WIN, WIN))
        return lax.dynamic_update_slice(gradient, current + contribution, (zero_start, row_start, col_start))

    gradient = lax.fori_loop(0, slot_total, accumulate, jnp.zeros_like(padded))
    return transmission + step_scale * gradient[:, HALO:HALO + NR, HALO:HALO + NC]
```

```python
import functools

import jax
import jax.numpy as jnp
import numpy as np
from jax import lax
from jax.experimental import pallas as pl
from jax.experimental.pallas import tpu as pltpu
from jax.sharding import PartitionSpec as P

HALO = 128
FLOOR_VALUE = 0.5
LANES = 128


def shifted(shard, axis, by):
    count = lax.axis_size(axis)
    pairs = [(i, i + by) for i in range(count) if 0 <= i + by < count]
    return lax.ppermute(shard, axis, pairs)


def tables(window):
    half = window // 2
    n = np.arange(half)
    k = np.arange(half)
    swapped = np.roll(k, -(half // 2))

    def real_form(frequency):
        angle = 2.0 * np.pi * ((n[:, None] * frequency[None, :]) % window) / window
        c = np.cos(angle) / np.sqrt(window)
        s = np.sin(angle) / np.sqrt(window)
        return np.block([[c, -s], [s, c]])

    def split(matrix):
        high = matrix.astype(np.float32).astype(jnp.bfloat16)
        low = (matrix - high.astype(np.float64)).astype(jnp.bfloat16)
        return np.stack([high, low])

    even, odd, odd_swapped = real_form(2 * k), real_form(2 * k + 1), real_form(2 * swapped + 1)
    return np.stack([split(m) for m in (even, odd_swapped, even.T, odd_swapped.T, odd.T, odd)])


def split_high_low(x):
    high = x.astype(jnp.bfloat16)
    low = (x - high.astype(jnp.float32)).astype(jnp.bfloat16)
    return high, low


def copies(pairs, sems):
    started = []
    for number, (source, target) in enumerate(pairs):
        copy = pltpu.make_async_copy(source, target, sems.at[number])
        copy.start()
        started.append(copy)
    return started


def process_slots(
    row_first, row_last, starts_ref, live_ref, scale_ref, probe_ref, tables_ref, amplitudes,
    extended, total, scratch,
):
    (probe_rolled, wave, side_even, side_odd, block_u, block_v) = scratch
    window = probe_ref.shape[1]
    half = window // 2
    slots = amplitudes.shape[0] // 2

    def chosen(index):
        subset = index // slots
        row = starts_ref[2 * index]
        return (index - subset * slots < live_ref[subset]) & (row >= row_first) & (row <= row_last)

    lane = lax.broadcasted_iota(jnp.int32, (half, LANES), 1)
    to_even_first = jnp.where(lane < half // 2, 2 * lane, 2 * lane - half + 1)
    to_odd_first = jnp.where(lane < half // 2, 2 * lane + 1, 2 * lane - half)
    lower = lane < half // 2

    def tall(block):
        high, low = block[:window], block[window:]
        return jnp.concatenate([high, high, low], axis=0)

    def wide(sides):
        high, low = sides[:, :window], sides[:, window:]
        return jnp.concatenate([high, high, low], axis=1)

    def right(sides, number):
        high, low = tables_ref[number, 0], tables_ref[number, 1]
        return jnp.dot(wide(sides), jnp.concatenate([high, low, high], axis=0),
                       preferred_element_type=jnp.float32)

    def left(number, block):
        high, low = tables_ref[number, 0], tables_ref[number, 1]
        return jnp.dot(jnp.concatenate([high, low, high], axis=1), tall(block),
                       preferred_element_type=jnp.float32)

    def process(index):
        row = starts_ref[2 * index]
        column = starts_ref[2 * index + 1]
        tile = column // LANES
        offset = column - tile * LANES
        last_tile = jnp.minimum(tile + 2, extended.shape[1] - 1)
        at = pl.ds(row, window)
        moved = lax.broadcasted_iota(jnp.int32, (window, LANES), 1) < offset

        for part in range(2):
            first = pltpu.roll(probe_ref[part, :, :LANES], offset, 1)
            second = pltpu.roll(probe_ref[part, :, LANES:], offset, 1)
            probe_rolled[part, 0] = jnp.where(moved, second, first)
            probe_rolled[part, 1] = jnp.where(moved, first, second)
        for side in range(2):
            if side == 0:
                view = [
                    jnp.where(moved, extended[p, last_tile, at, :], extended[p, tile, at, :])
                    for p in range(2)
                ]
            else:
                view = [extended[p, tile + 1, at, :] for p in range(2)]
            p_re, p_im = probe_rolled[0, side], probe_rolled[1, side]
            wave[0, side] = p_re * view[0] - p_im * view[1]
            wave[1, side] = p_re * view[1] + p_im * view[0]
        for part in range(2):
            for sides, sign in ((side_even, 1), (side_odd, -1)):
                x = wave[part, 0] + wave[part, 1] if sign > 0 else wave[part, 0] - wave[part, 1]
                high, low = split_high_low(x)
                sides[:, part * LANES:(part + 1) * LANES] = high
                sides[:, window + part * LANES:window + (part + 1) * LANES] = low
        for number, sides in ((0, side_even), (1, side_odd)):
            y = right(sides, number)
            upper, under = y[:half], y[half:]
            to = slice(number * LANES, (number + 1) * LANES)
            for block, x in ((block_u, upper + under), (block_v, upper - under)):
                high, low = split_high_low(x)
                for part in range(2):
                    lanes = slice(part * LANES, (part + 1) * LANES)
                    block[part * half:(part + 1) * half, to] = high[:, lanes]
                    block[window + part * half:window + (part + 1) * half, to] = low[:, lanes]

        for number, block in ((0, block_u), (1, block_v)):
            z = left(2 + 2 * number, block)
            z_re, z_im = z[:half], z[half:]
            picked = [amplitudes[index, t, pl.ds(number, half, stride=2), :] for t in range(2)]
            g0 = jnp.take_along_axis(picked[0], to_even_first, axis=1)
            g1 = jnp.take_along_axis(picked[1], to_odd_first, axis=1)
            for t, amplitude in ((0, jnp.where(lower, g0, g1)), (1, jnp.where(lower, g1, g0))):
                lanes = slice(t * LANES, (t + 1) * LANES)
                a, b = z_re[:, lanes], z_im[:, lanes]
                power = jnp.maximum(a * a + b * b, FLOOR_VALUE * FLOOR_VALUE)
                ratio = amplitude * lax.rsqrt(power)
                for part, x in ((0, a * ratio), (1, b * ratio)):
                    high, low = split_high_low(x)
                    block[part * half:(part + 1) * half, lanes] = high
                    block[window + part * half:window + (part + 1) * half, lanes] = low
        p, q = left(0, block_u), left(5, block_v)
        for rows_half, x in ((0, p + q), (1, p - q)):
            high, low = split_high_low(x)
            to = slice(rows_half * half, (rows_half + 1) * half)
            for number, sides in ((0, side_even), (1, side_odd)):
                lanes = slice(number * LANES, (number + 1) * LANES)
                for part in range(2):
                    of = slice(part * half, (part + 1) * half)
                    sides[to, part * LANES:(part + 1) * LANES] = high[of, lanes]
                    sides[to, window + part * LANES:window + (part + 1) * LANES] = low[of, lanes]
        p, q = right(side_even, 2), right(side_odd, 3)
        scale = scale_ref[:1]
        for side, x in ((0, p + q), (1, p - q)):
            d_re = (x[:, :LANES] - wave[0, side]) * scale
            d_im = (x[:, LANES:] - wave[1, side]) * scale
            p_re, p_im = probe_rolled[0, side], probe_rolled[1, side]
            g = (p_re * d_re + p_im * d_im, p_re * d_im - p_im * d_re)
            for part in range(2):
                if side == 0:
                    total[part, tile, at, :] += jnp.where(moved, 0.0, g[part])
                    total[part, last_tile, at, :] += jnp.where(moved, g[part], 0.0)
                else:
                    total[part, tile + 1, at, :] += g[part]

    def step(index, carry):
        @pl.when(chosen(index))
        def _():
            process(index)

        return carry

    lax.fori_loop(0, 2 * slots, step, 0)


def setup_kernel(
    center, measured_ref, probe_in, tables_in, extended, total, amplitudes, scale, probe, tables,
    sems,
):
    own = pl.ds(HALO, center.shape[1])
    tiles = extended.shape[1]
    subsets, slots = measured_ref.shape[2:4]
    started = copies(
        [(probe_in, probe)]
        + [(center.at[part, :, pl.ds(tile * LANES, LANES)], extended.at[part, tile + 1, own, :])
           for part in range(2) for tile in range(tiles - 2)]
        + [(tables_in, tables)]
        + [(measured_ref.at[0, 0, subset, slot, :, pl.ds(tile * LANES, LANES)],
            amplitudes.at[subset * slots + slot, tile])
           for subset in range(subsets) for slot in range(slots) for tile in range(2)],
        sems)
    total[...] = jnp.zeros_like(total)
    started[0].wait()
    squared = probe[0] * probe[0] + probe[1] * probe[1]
    scale[...] = jnp.broadcast_to(1.0 / jnp.max(squared, keepdims=True), scale.shape)
    for copy in started[1:]:
        copy.wait()


def slots_kernel(
    row_first, row_last, parts, outputs, starts_ref, live_ref, scale_ref, probe_ref, tables_ref,
    amplitudes, *refs,
):
    arrived, refs = refs[:len(parts)], refs[len(parts) + 2:]
    extended, total, *refs = refs
    outs, scratch = refs[:len(outputs)], refs[len(outputs):]
    for ref, (row, rows, first) in zip(arrived, parts):
        for part in range(2):
            for tile in range(ref.shape[2] // LANES):
                extended[part, first + tile, row:row + rows, :] = (
                    ref[part, :, tile * LANES:(tile + 1) * LANES])
    process_slots(row_first, row_last, starts_ref, live_ref, scale_ref, probe_ref, tables_ref,
                  amplitudes, extended, total, scratch)
    for ref, (row, rows, first, with_object) in zip(outs, outputs):
        for part in range(2):
            for tile in range(ref.shape[2] // LANES):
                value = total[part, first + tile, row:row + rows, :]
                if with_object:
                    value = value + extended[part, first + tile, row:row + rows, :]
                ref[part, :, tile * LANES:(tile + 1) * LANES] = value


SMEM = pl.BlockSpec(memory_space=pltpu.SMEM)
VMEM = pl.BlockSpec(memory_space=pltpu.VMEM)
ANY = pl.BlockSpec(memory_space=pl.ANY)
HBM = pl.BlockSpec(memory_space=pltpu.HBM)
MIB = 1024 * 1024


def run_slots(row_range, common, extended, total, arrived, parts, outputs, out_shapes):
    window = common[3].shape[1]
    f32, bf16 = jnp.float32, jnp.bfloat16
    n = len(common) + len(arrived)
    return pl.pallas_call(
        functools.partial(slots_kernel, *row_range, parts, outputs),
        out_shape=[pltpu.VMEM(shape, f32)
                   for shape in [extended.shape, total.shape] + out_shapes],
        in_specs=[SMEM, SMEM] + [VMEM] * (n),
        out_specs=[VMEM] * (2 + len(out_shapes)),
        input_output_aliases={n: 0, n + 1: 1},
        scratch_shapes=[
            pltpu.VMEM((2, 2, window, LANES), f32),
            pltpu.VMEM((2, 2, window, LANES), f32),
            pltpu.VMEM((window, 2 * window), bf16),
            pltpu.VMEM((window, 2 * window), bf16),
            pltpu.VMEM((2 * window, window), bf16),
            pltpu.VMEM((2 * window, window), bf16),
        ],
        compiler_params=pltpu.CompilerParams(vmem_limit_bytes=12 * MIB),
        cost_estimate=pl.CostEstimate(
            flops=4 * 24 * 2 * window ** 3, bytes_accessed=12 * MIB, transcendentals=0),
    )(*common, *arrived, extended, total)


def tail_kernel(body, from_left, from_right, from_below, out, head, kept, sems):
    height, width = body.shape[1:]
    kept[...] = body[...]
    kept[:, :, :HALO] += from_left[...]
    kept[:, :, width - HALO:] += from_right[...]
    kept[:, height - HALO:, :] += from_below[...]
    rows = pl.ds(HALO, height - HALO)
    started = copies([(kept.at[part, rows, :], out.at[part, rows, :]) for part in range(2)], sems)
    head[...] = kept[:, :HALO, :]
    for copy in started:
        copy.wait()


def head_kernel(head, from_above, old, out, kept, sems):
    kept[...] = head[...] + from_above[...]
    rows = pl.ds(0, HALO)
    for copy in copies([(kept.at[part], out.at[part, rows, :]) for part in range(2)], sems):
        copy.wait()


def update(transmission, probe_wave, positions, counts, measured):
    height, width = transmission.shape[1:]
    window = probe_wave.shape[1]
    slots = measured.shape[3]
    tiles = (width + 2 * HALO) // LANES
    whole = (2, tiles, height + 2 * HALO, LANES)
    wide_rim, small_rim, side = (2, HALO, width), (2, HALO, HALO), (2, height, HALO)
    above = shifted(transmission[:, height - HALO:, :], "narrow", 1)
    left = shifted(transmission[:, :, width - HALO:], "wide", 1)
    right = shifted(transmission[:, :, :HALO], "wide", -1)
    upper = transmission[:, :HALO, :]

    table = jnp.asarray(tables(window))
    f32 = jnp.float32
    loads = 2 + 2 * (tiles - 2) + 4 * slots
    extended, total, amplitudes, scale, probe, table = pl.pallas_call(
        setup_kernel, name="setup",
        out_shape=[
            pltpu.VMEM(whole, f32), pltpu.VMEM(whole, f32),
            pltpu.VMEM((2 * slots, 2, window, LANES), f32), pltpu.VMEM((8, LANES), f32),
            pltpu.VMEM(probe_wave.shape, f32), pltpu.VMEM(table.shape, table.dtype)],
        in_specs=[HBM] * 4, out_specs=[VMEM] * 6,
        scratch_shapes=[pltpu.SemaphoreType.DMA((loads,))],
        compiler_params=pltpu.CompilerParams(vmem_limit_bytes=12 * MIB),
        cost_estimate=pl.CostEstimate(
            flops=0, bytes_accessed=8 * MIB, transcendentals=0),
    )(*(pltpu.with_memory_space_constraint(x, pltpu.HBM)
        for x in (transmission, measured, probe_wave, table)))
    common = (positions.reshape(-1), counts.reshape(-1), scale, probe, table, amplitudes)

    extended, total = run_slots(
        (HALO, height + HALO - window), common, extended, total,
        (left, right), ((HALO, height, 0), (HALO, height, tiles - 1)), (), [])

    above, total, upper = lax.optimization_barrier((above, total, upper))
    below = shifted(upper, "narrow", -1)
    above_l = shifted(above[:, :, width - HALO:], "wide", 1)
    above_r = shifted(above[:, :, :HALO], "wide", -1)

    def rim(row):
        return ((row, HALO, 1), (row, HALO, 0), (row, HALO, tiles - 1))

    def rim_out(row):
        return tuple((*piece, False) for piece in rim(row))

    rims = [wide_rim, small_rim, small_rim]
    extended, total, up, up_l, up_r = run_slots(
        (0, HALO - 1), common, extended, total,
        (above, above_l, above_r), rim(0), rim_out(0), rims)

    def fold_columns(center, from_left, from_right):
        center = center.at[:, :, :HALO].add(from_left)
        return center.at[:, :, width - HALO:].add(from_right)

    up = fold_columns(up, shifted(up_r, "wide", 1), shifted(up_l, "wide", -1))
    from_below = shifted(up, "narrow", -1)

    below, total = lax.optimization_barrier((below, total))
    below_l = shifted(below[:, :, width - HALO:], "wide", 1)
    below_r = shifted(below[:, :, :HALO], "wide", -1)
    last = height + HALO
    extended, total, down, down_l, down_r, body, body_l, body_r = run_slots(
        (height + HALO - window + 1, height), common, extended, total,
        (below, below_l, below_r), rim(last),
        rim_out(last) + ((HALO, height, 1, True), (HALO, height, 0, False),
                         (HALO, height, tiles - 1, False)),
        rims + [(2, height, width), side, side])
    down = fold_columns(down, shifted(down_r, "wide", 1), shifted(down_l, "wide", -1))
    from_above = shifted(down, "narrow", 1)
    from_left = shifted(body_r, "wide", 1)
    from_right = shifted(body_l, "wide", -1)

    out, head = pl.pallas_call(
        tail_kernel, name="tail",
        out_shape=[jax.ShapeDtypeStruct((2, height, width), f32),
                   pltpu.VMEM(wide_rim, f32)],
        in_specs=[VMEM] * 4, out_specs=[ANY, VMEM],
        scratch_shapes=[pltpu.VMEM((2, height, width), f32), pltpu.SemaphoreType.DMA((2,))],
        compiler_params=pltpu.CompilerParams(vmem_limit_bytes=8 * MIB),
    )(body, from_left, from_right, from_below)
    return pl.pallas_call(
        head_kernel, name="head",
        out_shape=jax.ShapeDtypeStruct((2, height, width), f32),
        in_specs=[VMEM, VMEM, ANY], out_specs=ANY,
        input_output_aliases={2: 0},
        scratch_shapes=[pltpu.VMEM(wide_rim, f32), pltpu.SemaphoreType.DMA((2,))],
        compiler_params=pltpu.CompilerParams(vmem_limit_bytes=4 * MIB),
    )(head, from_above, out)


def solution(mesh):
    in_specs = (
        P(None, "narrow", "wide"),
        P(),
        P("narrow", "wide", None, None, None),
        P("narrow", "wide", None),
        P("narrow", "wide", None, None, None, None),
    )
    out_specs = P(None, "narrow", "wide")
    return jax.shard_map(update, mesh=mesh, in_specs=in_specs, out_specs=out_specs, check_vma=False)
```

```python
import functools

import jax
import jax.numpy as jnp
import numpy as np
from jax import lax
from jax.experimental import pallas as pl
from jax.experimental.pallas import tpu as pltpu
from jax.sharding import PartitionSpec as P

HALO = 128
FLOOR_VALUE = 0.5
LANES = 128
PIECE = 32
HEAD = 2
EARLY = 4


NEAR, FAR = range(2)


def swapped(shard, axis, which):
    count = lax.axis_size(axis)
    pairs = [pair for i in range(which, count - 1, 2) for pair in ((i, i + 1), (i + 1, i))]
    return lax.ppermute(shard, axis, pairs)


def is_after(axis, which):
    odd = lax.rem(lax.axis_index(axis), 2)
    return odd if which == FAR else 1 - odd


def tables(window):
    half = window // 2
    n = np.arange(half)
    k = np.arange(half)
    swapped = np.roll(k, -(half // 2))

    def real_form(frequency):
        angle = 2.0 * np.pi * ((n[:, None] * frequency[None, :]) % window) / window
        c = np.cos(angle) / np.sqrt(window)
        s = np.sin(angle) / np.sqrt(window)
        return np.block([[c, -s], [s, c]])

    def split(matrix):
        high = matrix.astype(np.float32).astype(jnp.bfloat16)
        low = (matrix - high.astype(np.float64)).astype(jnp.bfloat16)
        return np.stack([high, low])

    even, odd, odd_swapped = real_form(2 * k), real_form(2 * k + 1), real_form(2 * swapped + 1)
    return np.stack([split(m) for m in (even, odd, odd.T, odd_swapped)])


EVEN, ODD_SWAPPED, EVEN_T, ODD_SWAPPED_T, EVEN_T_PIECES, ODD_T_PIECES, ODD = range(7)


def place_tables(shipped, full):
    window = full.shape[2]
    half = window // 2
    quarter = half // 2
    for level in range(2):
        even, odd, odd_t, swapped = (shipped[number, level] for number in range(4))
        full[EVEN, level] = even
        full[ODD, level] = odd
        full[ODD_SWAPPED, level] = swapped
        even_t = jnp.concatenate([
            jnp.concatenate([even[:half, :half], even[half:, :half]], axis=1),
            jnp.concatenate([even[:half, half:], even[half:, half:]], axis=1)], axis=0)
        full[EVEN_T, level] = even_t
        for block in range(4):
            to = (block ^ 1) * quarter
            full[ODD_SWAPPED_T, level, to:to + quarter, :] = (
                odd_t[block * quarter:(block + 1) * quarter])
        for first in range(0, half, PIECE):
            for part in range(2):
                to = slice(2 * first + part * PIECE, 2 * first + (part + 1) * PIECE)
                of = slice(part * half + first, part * half + first + PIECE)
                full[EVEN_T_PIECES, level, to, :] = even_t[of]
                full[ODD_T_PIECES, level, to, :] = odd_t[of]


def split_high_low(x):
    high = x.astype(jnp.bfloat16)
    low = (x - high.astype(jnp.float32)).astype(jnp.bfloat16)
    return high, low


def copies(pairs, sems):
    started = []
    for number, (source, target) in enumerate(pairs):
        copy = pltpu.make_async_copy(source, target, sems.at[number])
        copy.start()
        started.append(copy)
    return started


def process_slots(
    first_part, early, plan_ref, scale_ref, probe_ref, tables_ref, amplitudes, extended, total,
    stages,
):
    window = probe_ref.shape[1]
    half = window // 2
    places = amplitudes.shape[0]

    pieces = []
    for first in range(0, half, PIECE):
        for at_half in range(2):
            begin = 2 * first + at_half * PIECE
            pieces.append((slice(begin, begin + PIECE),
                           slice(at_half * half + first, at_half * half + first + PIECE)))

    lane = lax.broadcasted_iota(jnp.int32, (PIECE, LANES), 1)
    to_even_first = jnp.where(lane < half // 2, 2 * lane, 2 * lane - half + 1)
    to_odd_first = jnp.where(lane < half // 2, 2 * lane + 1, 2 * lane - half)
    lower = lane < half // 2

    def tall(block):
        high, low = block[:window], block[window:]
        return jnp.concatenate([high, high, low], axis=0)

    def wide(sides):
        high, low = sides[:, :window], sides[:, window:]
        return jnp.concatenate([high, high, low], axis=1)

    def right(sides, number):
        high, low = tables_ref[number, 0], tables_ref[number, 1]
        return jnp.dot(wide(sides), jnp.concatenate([high, low, high], axis=0),
                       preferred_element_type=jnp.float32)

    def left(number, block):
        high, low = tables_ref[number, 0], tables_ref[number, 1]
        return jnp.dot(jnp.concatenate([high, low, high], axis=1), tall(block),
                       preferred_element_type=jnp.float32)

    def process(index, which):
        probe_rolled, wave, side_even, side_odd, block_u, block_v = (
            ref.at[which] for ref in stages)
        row = plan_ref[HEAD + places + 2 * index]
        column = plan_ref[HEAD + places + 2 * index + 1]
        tile = column // LANES
        offset = column - tile * LANES
        last_tile = jnp.minimum(tile + 2, extended.shape[1] - 1)
        at = pl.ds(row, window)
        moved = lax.broadcasted_iota(jnp.int32, (window, LANES), 1) < offset

        for part in range(2):
            first = pltpu.roll(probe_ref[part, :, :LANES], offset, 1)
            second = pltpu.roll(probe_ref[part, :, LANES:], offset, 1)
            probe_rolled[part, 0] = jnp.where(moved, second, first)
            probe_rolled[part, 1] = jnp.where(moved, first, second)
        for side in range(2):
            if side == 0:
                view = [
                    jnp.where(moved, extended[p, last_tile, at, :], extended[p, tile, at, :])
                    for p in range(2)
                ]
            else:
                view = [extended[p, tile + 1, at, :] for p in range(2)]
            p_re, p_im = probe_rolled[0, side], probe_rolled[1, side]
            wave[0, side] = p_re * view[0] - p_im * view[1]
            wave[1, side] = p_re * view[1] + p_im * view[0]
        yield
        for number, sides in ((0, side_even), (1, side_odd)):
            for part in range(2):
                x = wave[part, 0] + wave[part, 1] if number == 0 else wave[part, 0] - wave[part, 1]
                high, low = split_high_low(x)
                lanes = slice(part * LANES, (part + 1) * LANES)
                for to, of in pieces:
                    sides[to, lanes] = high[of]
                    sides[to, window + part * LANES:window + (part + 1) * LANES] = low[of]
            y = right(sides, EVEN if number == 0 else ODD_SWAPPED)
            yield
            to = slice(number * LANES, (number + 1) * LANES)
            for first in range(0, half, PIECE):
                upper = y[2 * first:2 * first + PIECE]
                under = y[2 * first + PIECE:2 * first + 2 * PIECE]
                for block, x in ((block_u, upper + under), (block_v, upper - under)):
                    high, low = split_high_low(x)
                    for part in range(2):
                        lanes = slice(part * LANES, (part + 1) * LANES)
                        row_at = part * half + first
                        block[row_at:row_at + PIECE, to] = high[:, lanes]
                        block[window + row_at:window + row_at + PIECE, to] = low[:, lanes]

            yield
        for number, block in ((0, block_u), (1, block_v)):
            z = left(EVEN_T_PIECES if number == 0 else ODD_T_PIECES, block)
            yield
            for first in range(0, half, PIECE):
                z_re = z[2 * first:2 * first + PIECE]
                z_im = z[2 * first + PIECE:2 * first + 2 * PIECE]
                picked = [
                    amplitudes[index, t, pl.ds(number + 2 * first, PIECE, stride=2), :]
                    for t in range(2)
                ]
                g0 = jnp.take_along_axis(picked[0], to_even_first, axis=1)
                g1 = jnp.take_along_axis(picked[1], to_odd_first, axis=1)
                for t, amplitude in ((0, jnp.where(lower, g0, g1)), (1, jnp.where(lower, g1, g0))):
                    lanes = slice(t * LANES, (t + 1) * LANES)
                    a, b = z_re[:, lanes], z_im[:, lanes]
                    power = jnp.maximum(a * a + b * b, FLOOR_VALUE * FLOOR_VALUE)
                    ratio = amplitude * lax.rsqrt(power)
                    for part, x in ((0, a * ratio), (1, b * ratio)):
                        high, low = split_high_low(x)
                        row_at = part * half + first
                        block[row_at:row_at + PIECE, lanes] = high
                        block[window + row_at:window + row_at + PIECE, lanes] = low
            yield
        p, q = left(EVEN, block_u), left(ODD, block_v)
        yield
        for rows_half, x in ((0, p + q), (1, p - q)):
            high, low = split_high_low(x)
            to = slice(rows_half * half, (rows_half + 1) * half)
            for number, sides in ((0, side_even), (1, side_odd)):
                lanes = slice(number * LANES, (number + 1) * LANES)
                for part in range(2):
                    of = slice(part * half, (part + 1) * half)
                    sides[to, part * LANES:(part + 1) * LANES] = high[of, lanes]
                    sides[to, window + part * LANES:window + (part + 1) * LANES] = low[of, lanes]
        yield
        p, q = right(side_even, EVEN_T), right(side_odd, ODD_SWAPPED_T)
        yield
        scale = scale_ref[:1]
        for side, x in ((0, p + q), (1, p - q)):
            d_re = (x[:, :LANES] - wave[0, side]) * scale
            d_im = (x[:, LANES:] - wave[1, side]) * scale
            p_re, p_im = probe_rolled[0, side], probe_rolled[1, side]
            g = (p_re * d_re + p_im * d_im, p_re * d_im - p_im * d_re)
            for part in range(2):
                if side == 0:
                    total[part, tile, at, :] += jnp.where(moved, 0.0, g[part])
                    total[part, last_tile, at, :] += jnp.where(moved, g[part], 0.0)
                else:
                    total[part, tile + 1, at, :] += g[part]

    split = jnp.minimum(plan_ref[0], early)
    begin, end = (0, split) if first_part else (split, plan_ref[1])
    count = end - begin

    def two(pair, carry):
        first = process(plan_ref[HEAD + begin + 2 * pair], 0)
        second = process(plan_ref[HEAD + begin + 2 * pair + 1], 1)
        next(first)
        for _ in second:
            next(first, None)
        return carry

    lax.fori_loop(0, count // 2, two, 0)

    @pl.when(count % 2 == 1)
    def _():
        for _ in process(plan_ref[HEAD + end - 1], 0):
            pass


def corners_kernel(center, near, far, sems):
    height, width = center.shape[1:]
    pairs = []
    for which, ref in ((NEAR, near), (FAR, far)):
        row = pl.multiple_of(is_after("narrow", which) * (height - HALO), HALO)
        for part in range(2):
            for to, lane in ((0, 0), (HALO, width - HALO)):
                pairs.append((center.at[part, pl.ds(row, HALO), pl.ds(lane, HALO)],
                              ref.at[part, :, pl.ds(to, HALO)]))
    for copy in copies(pairs, sems):
        copy.wait()


def edges_kernel(center, near_columns, far_columns, near_rows, far_rows, sems):
    height, width = center.shape[1:]
    pairs = []
    for which, columns, rows in ((NEAR, near_columns, near_rows), (FAR, far_columns, far_rows)):
        row = pl.multiple_of(is_after("narrow", which) * (height - HALO), HALO)
        lane = pl.multiple_of(is_after("wide", which) * (width - HALO), HALO)
        for part in range(2):
            pairs += [
                (center.at[part, :, pl.ds(lane, HALO)], columns.at[part]),
                (center.at[part, pl.ds(row, HALO), pl.ds(HALO, width - 2 * HALO)], rows.at[part]),
            ]
    for copy in copies(pairs, sems):
        copy.wait()


def setup_kernel(
    starts_in, live_in, center, measured_ref, probe_in, tables_in, extended, total, amplitudes,
    scale, probe, tables_full, plan, tables_got, starts_ref, live_ref, sems, amplitude_sems,
):
    own = pl.ds(HALO, center.shape[1])
    tiles = extended.shape[1]
    subsets, slots = measured_ref.shape[2:4]
    *small, = copies([(starts_in, starts_ref), (live_in, live_ref)], sems)
    started = copies(
        [(probe_in, probe), (tables_in, tables_got)]
        + [(center.at[part, :, pl.ds(tile * LANES, LANES)], extended.at[part, tile + 1, own, :])
           for part in range(2) for tile in range(tiles - 2)],
        sems.at[pl.ds(2, sems.shape[0] - 2)])
    for copy in small:
        copy.wait()

    def each_live(act):
        def one(number, carry):
            subset = number // slots
            slot = number - subset * slots

            @pl.when(slot < live_ref[0, 0, subset])
            def _():
                for tile in range(2):
                    act(pltpu.make_async_copy(
                        measured_ref.at[0, 0, subset, slot, :, pl.ds(tile * LANES, LANES)],
                        amplitudes.at[number, tile], amplitude_sems.at[number, tile]))

            return carry

        lax.fori_loop(0, subsets * slots, one, 0)

    each_live(lambda copy: copy.start())

    places = subsets * slots
    window = amplitudes.shape[2]
    last_inner = center.shape[1] + HALO - window

    def sort(inner, number, count):
        subset = number // slots
        slot = number - subset * slots
        row = starts_ref[0, 0, subset, 0, slot]
        inside = (row >= HALO) & (row <= last_inner)
        mine = (slot < live_ref[0, 0, subset]) & (inside == inner)

        @pl.when(mine)
        def _():
            plan[HEAD + count] = number

        if inner:
            for axis in range(2):
                plan[HEAD + places + 2 * number + axis] = starts_ref[0, 0, subset, axis, slot]
        return count + mine.astype(jnp.int32)

    inner_count = lax.fori_loop(0, places, functools.partial(sort, True), jnp.int32(0))
    plan[0] = inner_count
    plan[1] = lax.fori_loop(0, places, functools.partial(sort, False), inner_count)
    total[...] = jnp.zeros_like(total)
    started[0].wait()
    squared = probe[0] * probe[0] + probe[1] * probe[1]
    scale[...] = jnp.broadcast_to(1.0 / jnp.max(squared, keepdims=True), scale.shape)
    started[1].wait()
    place_tables(tables_got, tables_full)
    for copy in started[2:]:
        copy.wait()
    each_live(lambda copy: copy.wait())


def slots_kernel(
    n_in, n_out, first_part, early, parts, outputs, plan_ref, scale_ref, probe_ref, tables_ref,
    amplitudes, *refs,
):
    arrived, refs = refs[:n_in], refs[n_in + 2:]
    extended, total, *refs = refs
    outs, scratch = refs[:n_out], refs[n_out:]

    def place(key, end):
        return key if isinstance(key, int) else is_after(*key) * end

    def pieces(entries, arrays):
        for number, of, row, rows, tiles in entries:
            if not isinstance(row, int):
                row = pl.multiple_of(place(row, extended.shape[2] - HALO), HALO)
            for part in range(2):
                for lane, tile in enumerate(tiles):
                    yield (arrays[number],
                           (part, slice(of, of + rows), slice(lane * LANES, (lane + 1) * LANES)),
                           (part, place(tile, extended.shape[1] - 1), pl.ds(row, rows)))

    for ref, here, there in pieces(parts, arrived):
        extended[there] = ref[here]
    process_slots(first_part, early, plan_ref, scale_ref, probe_ref, tables_ref, amplitudes,
                  extended, total, scratch)
    for ref, here, there in pieces(outputs, outs):
        ref[here] = total[there]


SMEM = pl.BlockSpec(memory_space=pltpu.SMEM)
VMEM = pl.BlockSpec(memory_space=pltpu.VMEM)
ANY = pl.BlockSpec(memory_space=pl.ANY)
HBM = pl.BlockSpec(memory_space=pltpu.HBM)
MIB = 1024 * 1024


def run_slots(first_part, early, common, extended, total, arrived, parts, outputs, out_shapes):
    window = common[2].shape[1]
    f32, bf16 = jnp.float32, jnp.bfloat16
    n = len(common) + len(arrived)
    return pl.pallas_call(
        functools.partial(slots_kernel, len(arrived), len(out_shapes), first_part, early, parts,
                          outputs),
        out_shape=[pltpu.VMEM(shape, f32)
                   for shape in [extended.shape, total.shape] + out_shapes],
        in_specs=[SMEM] + [VMEM] * (n + 1),
        out_specs=[VMEM] * (2 + len(out_shapes)),
        input_output_aliases={n: 0, n + 1: 1},
        scratch_shapes=[
            pltpu.VMEM((2, 2, 2, window, LANES), f32),
            pltpu.VMEM((2, 2, 2, window, LANES), f32),
            pltpu.VMEM((2, window, 2 * window), bf16),
            pltpu.VMEM((2, window, 2 * window), bf16),
            pltpu.VMEM((2, 2 * window, window), bf16),
            pltpu.VMEM((2, 2 * window, window), bf16),
        ],
        compiler_params=pltpu.CompilerParams(vmem_limit_bytes=12 * MIB),
        cost_estimate=pl.CostEstimate(
            flops=4 * 24 * 2 * window ** 3, bytes_accessed=12 * MIB, transcendentals=0),
    )(*common, *arrived, extended, total)


def sides(axis, near, far):
    near_after = is_after(axis, NEAR) == 1
    return jnp.where(near_after, far, near), jnp.where(near_after, near, far)


def ends_kernel(near_outer, far_outer, near, far):
    for which, ref in ((NEAR, near), (FAR, far)):
        after = is_after("wide", which) == 1
        for number, rim in enumerate((near_outer, far_outer)):
            ref[:, number * HALO:(number + 1) * HALO, :] = jnp.where(
                after, rim[:, :, HALO:], rim[:, :, :HALO])


def folded_kernel(near_ends, far_ends, near_rim, far_rim, near, far):
    left, right = sides("wide", near_rim[...], far_rim[...])
    for number, (ref, ends) in enumerate(((near, near_ends), (far, far_ends))):
        rows = slice(number * HALO, (number + 1) * HALO)
        ref[:, :, :HALO] = ends[:, :, :HALO] + left[:, rows]
        ref[:, :, HALO:] = ends[:, :, HALO:] + right[:, rows]


def tail_kernel(
    extended, total, near_side, far_side, near_middle, far_middle, out, head, foot, kept, sems,
):
    height, width = kept.shape[1:]
    own = slice(HALO, HALO + height)
    for part in range(2):
        for tile in range(width // LANES):
            kept[part, :, tile * LANES:(tile + 1) * LANES] = (
                extended[part, tile + 1, own, :] + total[part, tile + 1, own, :])
        left, right = sides("wide", near_side[part], far_side[part])
        kept[part, :, :HALO] += left
        kept[part, :, width - HALO:] += right
        above, below = sides("narrow", near_middle[part], far_middle[part])
        kept[part, :HALO, HALO:width - HALO] += above
        kept[part, height - HALO:, HALO:width - HALO] += below
    rows = pl.ds(HALO, height - 2 * HALO)
    started = copies([(kept.at[part, rows, :], out.at[part, rows, :]) for part in range(2)], sems)
    head[...] = kept[:, :HALO, :]
    foot[...] = kept[:, height - HALO:, :]
    for copy in started:
        copy.wait()


def rims_kernel(head, foot, near_outer, far_outer, old, out, head_kept, foot_kept, sems):
    height, width = out.shape[1:]
    started = []
    outer = sides("narrow", near_outer[...], far_outer[...])
    for number, (ref, kept, row) in enumerate((
        (head, head_kept, 0), (foot, foot_kept, height - HALO),
    )):
        kept[...] = ref[...]
        kept[:, :, :HALO] += outer[number][:, :, :HALO]
        kept[:, :, width - HALO:] += outer[number][:, :, HALO:]
        started += copies(
            [(kept.at[part], out.at[part, pl.ds(row, HALO), :]) for part in range(2)],
            sems.at[pl.ds(2 * number, 2)])
    for copy in started:
        copy.wait()


def update(transmission, probe_wave, positions, counts, measured):
    height, width = transmission.shape[1:]
    window = probe_wave.shape[1]
    slots = measured.shape[3]
    tiles = (width + 2 * HALO) // LANES
    whole = (2, tiles, height + 2 * HALO, LANES)
    wide_rim, side = (2, HALO, width), (2, height, HALO)
    outer, middle = (2, HALO, 2 * HALO), (2, HALO, width - 2 * HALO)
    f32 = jnp.float32
    transmission = pltpu.with_memory_space_constraint(transmission, pltpu.HBM)
    near_outer, far_outer = pl.pallas_call(
        corners_kernel, name="corners",
        out_shape=[pltpu.VMEM(outer, f32)] * 2,
        in_specs=[HBM], out_specs=[VMEM] * 2,
        scratch_shapes=[pltpu.SemaphoreType.DMA((8,))],
        compiler_params=pltpu.CompilerParams(vmem_limit_bytes=4 * MIB),
    )(transmission)

    def exchange(axis, near, far):
        from_far = swapped(far, axis, FAR)
        return swapped(near, axis, NEAR), from_far

    near_outer, far_outer = exchange("narrow", near_outer, far_outer)
    near_columns, far_columns, near_middle, far_middle = pl.pallas_call(
        edges_kernel, name="edges",
        out_shape=[pltpu.VMEM(shape, f32) for shape in (side, side, middle, middle)],
        in_specs=[HBM], out_specs=[VMEM] * 4,
        scratch_shapes=[pltpu.SemaphoreType.DMA((8,))],
        compiler_params=pltpu.CompilerParams(vmem_limit_bytes=4 * MIB),
    )(transmission)
    near_columns, far_columns = exchange("wide", near_columns, far_columns)

    table = jnp.asarray(tables(window))
    extended, total, amplitudes, scale, probe, full, plan = pl.pallas_call(
        setup_kernel, name="setup",
        out_shape=[
            pltpu.VMEM(whole, f32), pltpu.VMEM(whole, f32),
            pltpu.VMEM((2 * slots, 2, window, LANES), f32), pltpu.VMEM((8, LANES), f32),
            pltpu.VMEM(probe_wave.shape, f32),
            pltpu.VMEM((7, *table.shape[1:]), table.dtype),
            jax.ShapeDtypeStruct((HEAD + 6 * slots,), jnp.int32)],
        in_specs=[HBM] * 6, out_specs=[VMEM] * 6 + [SMEM],
        scratch_shapes=[
            pltpu.VMEM(table.shape, table.dtype),
            pltpu.SMEM((1, 1, 2, 2, slots), jnp.int32), pltpu.SMEM(counts.shape, jnp.int32),
            pltpu.SemaphoreType.DMA((4 + 2 * (tiles - 2),)),
            pltpu.SemaphoreType.DMA((2 * slots, 2))],
        compiler_params=pltpu.CompilerParams(vmem_limit_bytes=12 * MIB),
        cost_estimate=pl.CostEstimate(
            flops=0, bytes_accessed=8 * MIB, transcendentals=0),
    )(*(pltpu.with_memory_space_constraint(x, pltpu.HBM)
        for x in (jnp.swapaxes(positions, 3, 4), counts, transmission, measured, probe_wave,
                  table)))
    common = (plan, scale, probe, full, amplitudes)
    near_middle, far_middle = exchange("narrow", near_middle, far_middle)

    def small_kernel(kernel, outs, *ins):
        return pl.pallas_call(
            kernel,
            out_shape=[pltpu.VMEM(shape, f32) for shape in outs],
            in_specs=[VMEM] * len(ins), out_specs=[VMEM] * len(outs),
            compiler_params=pltpu.CompilerParams(vmem_limit_bytes=4 * MIB),
        )(*ins)

    both = (2, 2 * HALO, HALO)
    near_corner, far_corner = exchange(
        "wide", *small_kernel(ends_kernel, [both] * 2, near_outer, far_outer))

    inner_tiles, ends = tuple(range(2, tiles - 2)), (1, tiles - 2)
    beside = (("wide", NEAR),), (("wide", FAR),)
    near_row, far_row = ("narrow", NEAR), ("narrow", FAR)
    extended, total = run_slots(
        True, EARLY, common, extended, total,
        (near_columns, far_columns),
        ((NEAR, 0, HALO, height, beside[NEAR]), (FAR, 0, HALO, height, beside[FAR])), (), [])
    rows_in = (
        (0, 0, near_row, HALO, inner_tiles), (1, 0, far_row, HALO, inner_tiles),
        (2, 0, near_row, HALO, ends), (3, 0, far_row, HALO, ends),
        *((4 + which, of, row, HALO, beside[which])
          for which in (NEAR, FAR) for of, row in ((0, near_row), (HALO, far_row))))
    (extended, total, near_up, far_up, near_ends, far_ends, near_rim, far_rim, near_side,
     far_side) = run_slots(
        False, EARLY, common, extended, total,
        (near_middle, far_middle, near_outer, far_outer, near_corner, far_corner), rows_in,
        rows_in + ((6, 0, HALO, height, beside[NEAR]), (7, 0, HALO, height, beside[FAR])),
        [middle, middle, outer, outer, both, both, side, side])
    near_up, far_up = exchange("narrow", near_up, far_up)
    near_rim, far_rim = exchange("wide", near_rim, far_rim)

    near_ends, far_ends = exchange(
        "narrow", *small_kernel(
            folded_kernel, [outer] * 2, near_ends, far_ends, near_rim, far_rim))
    near_side, far_side = exchange("wide", near_side, far_side)

    out, head, foot = pl.pallas_call(
        tail_kernel, name="tail",
        out_shape=[jax.ShapeDtypeStruct((2, height, width), f32),
                   pltpu.VMEM(wide_rim, f32), pltpu.VMEM(wide_rim, f32)],
        in_specs=[VMEM] * 6, out_specs=[ANY, VMEM, VMEM],
        scratch_shapes=[pltpu.VMEM((2, height, width), f32), pltpu.SemaphoreType.DMA((2,))],
        compiler_params=pltpu.CompilerParams(vmem_limit_bytes=8 * MIB),
    )(extended, total, near_side, far_side, near_up, far_up)
    return pl.pallas_call(
        rims_kernel, name="rims",
        out_shape=jax.ShapeDtypeStruct((2, height, width), f32),
        in_specs=[VMEM] * 4 + [ANY], out_specs=ANY,
        input_output_aliases={4: 0},
        scratch_shapes=[pltpu.VMEM(wide_rim, f32), pltpu.VMEM(wide_rim, f32),
                        pltpu.SemaphoreType.DMA((4,))],
        compiler_params=pltpu.CompilerParams(vmem_limit_bytes=4 * MIB),
    )(head, foot, near_ends, far_ends, out)


def solution(mesh):
    in_specs = (
        P(None, "narrow", "wide"),
        P(),
        P("narrow", "wide", None, None, None),
        P("narrow", "wide", None),
        P("narrow", "wide", None, None, None, None),
    )
    out_specs = P(None, "narrow", "wide")
    return jax.shard_map(update, mesh=mesh, in_specs=in_specs, out_specs=out_specs, check_vma=False)
```

```python
import functools

import jax
import jax.numpy as jnp
import numpy as np
from jax import lax
from jax.experimental import pallas as pl
from jax.experimental.pallas import tpu as pltpu
from jax.sharding import PartitionSpec as P

HALO = 128
FLOOR_VALUE = 0.5
LANES = 128
PIECE = 32
HEAD = 2
EARLY = 4


NEAR, FAR = range(2)


def swapped(shard, axis, which):
    count = lax.axis_size(axis)
    pairs = [pair for i in range(which, count - 1, 2) for pair in ((i, i + 1), (i + 1, i))]
    return lax.ppermute(shard, axis, pairs)


def is_after(axis, which):
    odd = lax.rem(lax.axis_index(axis), 2)
    return odd if which == FAR else 1 - odd


def tables(window):
    half = window // 2
    n = np.arange(half)
    k = np.arange(half)
    swapped = np.roll(k, -(half // 2))

    def real_form(frequency):
        angle = 2.0 * np.pi * ((n[:, None] * frequency[None, :]) % window) / window
        c = np.cos(angle) / np.sqrt(window)
        s = np.sin(angle) / np.sqrt(window)
        return np.block([[c, -s], [s, c]])

    def split(matrix):
        high = matrix.astype(np.float32).astype(jnp.bfloat16)
        low = (matrix - high.astype(np.float64)).astype(jnp.bfloat16)
        return np.stack([high, low])

    even, odd, odd_swapped = real_form(2 * k), real_form(2 * k + 1), real_form(2 * swapped + 1)
    return np.stack([split(m) for m in (even, odd, odd.T, odd_swapped)])


EVEN, ODD_SWAPPED, EVEN_T, ODD_SWAPPED_T, EVEN_T_PIECES, ODD_T_PIECES, ODD = range(7)


def place_tables(shipped, full):
    window = full.shape[2]
    half = window // 2
    quarter = half // 2
    for level in range(2):
        even, odd, odd_t, swapped = (shipped[number, level] for number in range(4))
        full[EVEN, level] = even
        full[ODD, level] = odd
        full[ODD_SWAPPED, level] = swapped
        even_t = jnp.concatenate([
            jnp.concatenate([even[:half, :half], even[half:, :half]], axis=1),
            jnp.concatenate([even[:half, half:], even[half:, half:]], axis=1)], axis=0)
        full[EVEN_T, level] = even_t
        for block in range(4):
            to = (block ^ 1) * quarter
            full[ODD_SWAPPED_T, level, to:to + quarter, :] = (
                odd_t[block * quarter:(block + 1) * quarter])
        for first in range(0, half, PIECE):
            for part in range(2):
                to = slice(2 * first + part * PIECE, 2 * first + (part + 1) * PIECE)
                of = slice(part * half + first, part * half + first + PIECE)
                full[EVEN_T_PIECES, level, to, :] = even_t[of]
                full[ODD_T_PIECES, level, to, :] = odd_t[of]


def split_high_low(x):
    high = x.astype(jnp.bfloat16)
    low = (x - high.astype(jnp.float32)).astype(jnp.bfloat16)
    return high, low


def copies(pairs, sems):
    started = []
    for number, (source, target) in enumerate(pairs):
        copy = pltpu.make_async_copy(source, target, sems.at[number])
        copy.start()
        started.append(copy)
    return started


def process_slots(
    first_part, plan_ref, scale_ref, probe_ref, tables_ref, amplitudes, extended, total, stages,
):
    window = probe_ref.shape[1]
    half = window // 2
    places = amplitudes.shape[0]

    pieces = []
    for first in range(0, half, PIECE):
        for at_half in range(2):
            begin = 2 * first + at_half * PIECE
            pieces.append((slice(begin, begin + PIECE),
                           slice(at_half * half + first, at_half * half + first + PIECE)))

    lane = lax.broadcasted_iota(jnp.int32, (PIECE, LANES), 1)
    to_even_first = jnp.where(lane < half // 2, 2 * lane, 2 * lane - half + 1)
    to_odd_first = jnp.where(lane < half // 2, 2 * lane + 1, 2 * lane - half)
    lower = lane < half // 2

    def tall(block):
        high, low = block[:window], block[window:]
        return jnp.concatenate([high, high, low], axis=0)

    def wide(sides):
        high, low = sides[:, :window], sides[:, window:]
        return jnp.concatenate([high, high, low], axis=1)

    def right(sides, number):
        high, low = tables_ref[number, 0], tables_ref[number, 1]
        return jnp.dot(wide(sides), jnp.concatenate([high, low, high], axis=0),
                       preferred_element_type=jnp.float32)

    def left(number, block):
        high, low = tables_ref[number, 0], tables_ref[number, 1]
        return jnp.dot(jnp.concatenate([high, low, high], axis=1), tall(block),
                       preferred_element_type=jnp.float32)

    def process(index, which):
        probe_rolled, wave, side_even, side_odd, block_u, block_v = (
            ref.at[which] for ref in stages)
        row = plan_ref[HEAD + places + 2 * index]
        column = plan_ref[HEAD + places + 2 * index + 1]
        tile = column // LANES
        offset = column - tile * LANES
        last_tile = jnp.minimum(tile + 2, extended.shape[1] - 1)
        at = pl.ds(row, window)
        moved = lax.broadcasted_iota(jnp.int32, (window, LANES), 1) < offset

        for part in range(2):
            first = pltpu.roll(probe_ref[part, :, :LANES], offset, 1)
            second = pltpu.roll(probe_ref[part, :, LANES:], offset, 1)
            probe_rolled[part, 0] = jnp.where(moved, second, first)
            probe_rolled[part, 1] = jnp.where(moved, first, second)
        for side in range(2):
            if side == 0:
                view = [
                    jnp.where(moved, extended[p, last_tile, at, :], extended[p, tile, at, :])
                    for p in range(2)
                ]
            else:
                view = [extended[p, tile + 1, at, :] for p in range(2)]
            p_re, p_im = probe_rolled[0, side], probe_rolled[1, side]
            wave[0, side] = p_re * view[0] - p_im * view[1]
            wave[1, side] = p_re * view[1] + p_im * view[0]
        yield
        for number, sides in ((0, side_even), (1, side_odd)):
            for part in range(2):
                x = wave[part, 0] + wave[part, 1] if number == 0 else wave[part, 0] - wave[part, 1]
                high, low = split_high_low(x)
                lanes = slice(part * LANES, (part + 1) * LANES)
                for to, of in pieces:
                    sides[to, lanes] = high[of]
                    sides[to, window + part * LANES:window + (part + 1) * LANES] = low[of]
            y = right(sides, EVEN if number == 0 else ODD_SWAPPED)
            yield
            to = slice(number * LANES, (number + 1) * LANES)
            for first in range(0, half, PIECE):
                upper = y[2 * first:2 * first + PIECE]
                under = y[2 * first + PIECE:2 * first + 2 * PIECE]
                for block, x in ((block_u, upper + under), (block_v, upper - under)):
                    high, low = split_high_low(x)
                    for part in range(2):
                        lanes = slice(part * LANES, (part + 1) * LANES)
                        row_at = part * half + first
                        block[row_at:row_at + PIECE, to] = high[:, lanes]
                        block[window + row_at:window + row_at + PIECE, to] = low[:, lanes]

            yield
        for number, block in ((0, block_u), (1, block_v)):
            z = left(EVEN_T_PIECES if number == 0 else ODD_T_PIECES, block)
            yield
            for first in range(0, half, PIECE):
                z_re = z[2 * first:2 * first + PIECE]
                z_im = z[2 * first + PIECE:2 * first + 2 * PIECE]
                picked = [
                    amplitudes[index, t, pl.ds(number + 2 * first, PIECE, stride=2), :]
                    for t in range(2)
                ]
                g0 = jnp.take_along_axis(picked[0], to_even_first, axis=1)
                g1 = jnp.take_along_axis(picked[1], to_odd_first, axis=1)
                for t, amplitude in ((0, jnp.where(lower, g0, g1)), (1, jnp.where(lower, g1, g0))):
                    lanes = slice(t * LANES, (t + 1) * LANES)
                    a, b = z_re[:, lanes], z_im[:, lanes]
                    power = jnp.maximum(a * a + b * b, FLOOR_VALUE * FLOOR_VALUE)
                    ratio = amplitude * lax.rsqrt(power)
                    for part, x in ((0, a * ratio), (1, b * ratio)):
                        high, low = split_high_low(x)
                        row_at = part * half + first
                        block[row_at:row_at + PIECE, lanes] = high
                        block[window + row_at:window + row_at + PIECE, lanes] = low
            yield
        p, q = left(EVEN, block_u), left(ODD, block_v)
        yield
        for rows_half, x in ((0, p + q), (1, p - q)):
            high, low = split_high_low(x)
            to = slice(rows_half * half, (rows_half + 1) * half)
            for number, sides in ((0, side_even), (1, side_odd)):
                lanes = slice(number * LANES, (number + 1) * LANES)
                for part in range(2):
                    of = slice(part * half, (part + 1) * half)
                    sides[to, part * LANES:(part + 1) * LANES] = high[of, lanes]
                    sides[to, window + part * LANES:window + (part + 1) * LANES] = low[of, lanes]
        yield
        p, q = right(side_even, EVEN_T), right(side_odd, ODD_SWAPPED_T)
        yield
        scale = scale_ref[:1]
        for side, x in ((0, p + q), (1, p - q)):
            d_re = (x[:, :LANES] - wave[0, side]) * scale
            d_im = (x[:, LANES:] - wave[1, side]) * scale
            p_re, p_im = probe_rolled[0, side], probe_rolled[1, side]
            g = (p_re * d_re + p_im * d_im, p_re * d_im - p_im * d_re)
            for part in range(2):
                if side == 0:
                    total[part, tile, at, :] += jnp.where(moved, 0.0, g[part])
                    total[part, last_tile, at, :] += jnp.where(moved, g[part], 0.0)
                else:
                    total[part, tile + 1, at, :] += g[part]

    split = plan_ref[0]
    begin, end = (0, split) if first_part else (split, plan_ref[1])
    count = end - begin

    def two(pair, carry):
        first = process(plan_ref[HEAD + begin + 2 * pair], 0)
        second = process(plan_ref[HEAD + begin + 2 * pair + 1], 1)
        next(first)
        for _ in second:
            next(first, None)
        return carry

    lax.fori_loop(0, count // 2, two, 0)

    @pl.when(count % 2 == 1)
    def _():
        for _ in process(plan_ref[HEAD + end - 1], 0):
            pass


def corners_kernel(center, near, far, sems):
    height, width = center.shape[1:]
    pairs = []
    for which, ref in ((NEAR, near), (FAR, far)):
        row = pl.multiple_of(is_after("narrow", which) * (height - HALO), HALO)
        for part in range(2):
            for to, lane in ((0, 0), (HALO, width - HALO)):
                pairs.append((center.at[part, pl.ds(row, HALO), pl.ds(lane, HALO)],
                              ref.at[part, :, pl.ds(to, HALO)]))
    for copy in copies(pairs, sems):
        copy.wait()


def edges_kernel(center, near_columns, far_columns, near_rows, far_rows, sems):
    height, width = center.shape[1:]
    pairs = []
    for which, columns, rows in ((NEAR, near_columns, near_rows), (FAR, far_columns, far_rows)):
        row = pl.multiple_of(is_after("narrow", which) * (height - HALO), HALO)
        lane = pl.multiple_of(is_after("wide", which) * (width - HALO), HALO)
        for part in range(2):
            pairs += [
                (center.at[part, :, pl.ds(lane, HALO)], columns.at[part]),
                (center.at[part, pl.ds(row, HALO), pl.ds(HALO, width - 2 * HALO)], rows.at[part]),
            ]
    for copy in copies(pairs, sems):
        copy.wait()


def setup_kernel(
    starts_in, live_in, center, measured_ref, probe_in, tables_in, extended, total, amplitudes,
    scale, probe, tables_full, plan, tables_got, starts_ref, live_ref, sems, amplitude_sems,
):
    own = pl.ds(HALO, center.shape[1])
    tiles = extended.shape[1]
    subsets, slots = measured_ref.shape[2:4]
    *small, = copies([(starts_in, starts_ref), (live_in, live_ref)], sems)
    started = copies(
        [(probe_in, probe), (tables_in, tables_got)]
        + [(center.at[part, :, pl.ds(tile * LANES, LANES)], extended.at[part, tile + 1, own, :])
           for part in range(2) for tile in range(tiles - 2)],
        sems.at[pl.ds(2, sems.shape[0] - 2)])
    for copy in small:
        copy.wait()

    def each_live(act):
        def one(number, carry):
            subset = number // slots
            slot = number - subset * slots

            @pl.when(slot < live_ref[0, 0, subset])
            def _():
                for tile in range(2):
                    act(pltpu.make_async_copy(
                        measured_ref.at[0, 0, subset, slot, :, pl.ds(tile * LANES, LANES)],
                        amplitudes.at[number, tile], amplitude_sems.at[number, tile]))

            return carry

        lax.fori_loop(0, subsets * slots, one, 0)

    each_live(lambda copy: copy.start())

    places = subsets * slots
    window = amplitudes.shape[2]
    last_inner = center.shape[1] + HALO - window
    near_after = is_after("narrow", NEAR) == 1

    def sort(kind, number, count):
        subset = number // slots
        slot = number - subset * slots
        row = starts_ref[0, 0, subset, 0, slot]
        above, below = row < HALO, row > last_inner
        near = (near_after & below) | (jnp.logical_not(near_after) & above)
        inner = (row >= HALO) & (row <= last_inner)
        wanted = (near, inner, jnp.logical_not(near | inner))[kind]
        mine = (slot < live_ref[0, 0, subset]) & wanted

        @pl.when(mine)
        def _():
            plan[HEAD + count] = number

        if kind == 0:
            for axis in range(2):
                plan[HEAD + places + 2 * number + axis] = starts_ref[0, 0, subset, axis, slot]
        return count + mine.astype(jnp.int32)

    counts = [jnp.int32(0)]
    for kind in range(3):
        counts.append(lax.fori_loop(0, places, functools.partial(sort, kind), counts[-1]))
    plan[0] = jnp.maximum(counts[1], jnp.minimum(counts[2], EARLY))
    plan[1] = counts[3]
    total[...] = jnp.zeros_like(total)
    started[0].wait()
    squared = probe[0] * probe[0] + probe[1] * probe[1]
    scale[...] = jnp.broadcast_to(1.0 / jnp.max(squared, keepdims=True), scale.shape)
    started[1].wait()
    place_tables(tables_got, tables_full)
    for copy in started[2:]:
        copy.wait()
    each_live(lambda copy: copy.wait())


def slots_kernel(
    n_in, n_out, first_part, parts, outputs, plan_ref, scale_ref, probe_ref, tables_ref,
    amplitudes, *refs,
):
    arrived, refs = refs[:n_in], refs[n_in + 2:]
    extended, total, *refs = refs
    outs, scratch = refs[:n_out], refs[n_out:]

    def place(key, end):
        return key if isinstance(key, int) else is_after(*key) * end

    def pieces(entries, arrays):
        for number, of, row, rows, tiles in entries:
            if not isinstance(row, int):
                row = pl.multiple_of(place(row, extended.shape[2] - HALO), HALO)
            for part in range(2):
                for lane, tile in enumerate(tiles):
                    yield (arrays[number],
                           (part, slice(of, of + rows), slice(lane * LANES, (lane + 1) * LANES)),
                           (part, place(tile, extended.shape[1] - 1), pl.ds(row, rows)))

    for ref, here, there in pieces(parts, arrived):
        extended[there] = ref[here]
    process_slots(first_part, plan_ref, scale_ref, probe_ref, tables_ref, amplitudes,
                  extended, total, scratch)
    for ref, here, there in pieces(outputs, outs):
        ref[here] = total[there]


SMEM = pl.BlockSpec(memory_space=pltpu.SMEM)
VMEM = pl.BlockSpec(memory_space=pltpu.VMEM)
ANY = pl.BlockSpec(memory_space=pl.ANY)
HBM = pl.BlockSpec(memory_space=pltpu.HBM)
MIB = 1024 * 1024


def run_slots(first_part, common, extended, total, arrived, parts, outputs, out_shapes):
    window = common[2].shape[1]
    f32, bf16 = jnp.float32, jnp.bfloat16
    n = len(common) + len(arrived)
    return pl.pallas_call(
        functools.partial(slots_kernel, len(arrived), len(out_shapes), first_part, parts,
                          outputs),
        out_shape=[pltpu.VMEM(shape, f32)
                   for shape in [extended.shape, total.shape] + out_shapes],
        in_specs=[SMEM] + [VMEM] * (n + 1),
        out_specs=[VMEM] * (2 + len(out_shapes)),
        input_output_aliases={n: 0, n + 1: 1},
        scratch_shapes=[
            pltpu.VMEM((2, 2, 2, window, LANES), f32),
            pltpu.VMEM((2, 2, 2, window, LANES), f32),
            pltpu.VMEM((2, window, 2 * window), bf16),
            pltpu.VMEM((2, window, 2 * window), bf16),
            pltpu.VMEM((2, 2 * window, window), bf16),
            pltpu.VMEM((2, 2 * window, window), bf16),
        ],
        compiler_params=pltpu.CompilerParams(vmem_limit_bytes=12 * MIB),
        cost_estimate=pl.CostEstimate(
            flops=4 * 24 * 2 * window ** 3, bytes_accessed=12 * MIB, transcendentals=0),
    )(*common, *arrived, extended, total)


def sides(axis, near, far):
    near_after = is_after(axis, NEAR) == 1
    return jnp.where(near_after, far, near), jnp.where(near_after, near, far)


def ends_kernel(near_outer, far_outer, near, far):
    for which, ref in ((NEAR, near), (FAR, far)):
        after = is_after("wide", which) == 1
        for number, rim in enumerate((near_outer, far_outer)):
            ref[:, number * HALO:(number + 1) * HALO, :] = jnp.where(
                after, rim[:, :, HALO:], rim[:, :, :HALO])


def folded_kernel(ends, near_rim, far_rim, out):
    left, right = sides("wide", near_rim[...], far_rim[...])
    out[:, :, :HALO] = ends[:, :, :HALO] + left
    out[:, :, HALO:] = ends[:, :, HALO:] + right


def tail_kernel(
    extended, total, near_side, far_side, near_middle, far_middle, out, head, foot, kept, sems,
):
    height, width = kept.shape[1:]
    own = slice(HALO, HALO + height)
    for part in range(2):
        for tile in range(width // LANES):
            kept[part, :, tile * LANES:(tile + 1) * LANES] = (
                extended[part, tile + 1, own, :] + total[part, tile + 1, own, :])
        left, right = sides("wide", near_side[part], far_side[part])
        kept[part, :, :HALO] += left
        kept[part, :, width - HALO:] += right
        above, below = sides("narrow", near_middle[part], far_middle[part])
        kept[part, :HALO, HALO:width - HALO] += above
        kept[part, height - HALO:, HALO:width - HALO] += below
    rows = pl.ds(HALO, height - 2 * HALO)
    started = copies([(kept.at[part, rows, :], out.at[part, rows, :]) for part in range(2)], sems)
    head[...] = kept[:, :HALO, :]
    foot[...] = kept[:, height - HALO:, :]
    for copy in started:
        copy.wait()


def rims_kernel(head, foot, near_outer, far_outer, old, out, head_kept, foot_kept, sems):
    height, width = out.shape[1:]
    started = []
    outer = sides("narrow", near_outer[...], far_outer[...])
    for number, (ref, kept, row) in enumerate((
        (head, head_kept, 0), (foot, foot_kept, height - HALO),
    )):
        kept[...] = ref[...]
        kept[:, :, :HALO] += outer[number][:, :, :HALO]
        kept[:, :, width - HALO:] += outer[number][:, :, HALO:]
        started += copies(
            [(kept.at[part], out.at[part, pl.ds(row, HALO), :]) for part in range(2)],
            sems.at[pl.ds(2 * number, 2)])
    for copy in started:
        copy.wait()


def update(transmission, probe_wave, positions, counts, measured):
    height, width = transmission.shape[1:]
    window = probe_wave.shape[1]
    slots = measured.shape[3]
    tiles = (width + 2 * HALO) // LANES
    whole = (2, tiles, height + 2 * HALO, LANES)
    wide_rim, small_rim, side = (2, HALO, width), (2, HALO, HALO), (2, height, HALO)
    outer, middle = (2, HALO, 2 * HALO), (2, HALO, width - 2 * HALO)
    f32 = jnp.float32
    transmission = pltpu.with_memory_space_constraint(transmission, pltpu.HBM)
    near_outer, far_outer = pl.pallas_call(
        corners_kernel, name="corners",
        out_shape=[pltpu.VMEM(outer, f32)] * 2,
        in_specs=[HBM], out_specs=[VMEM] * 2,
        scratch_shapes=[pltpu.SemaphoreType.DMA((8,))],
        compiler_params=pltpu.CompilerParams(vmem_limit_bytes=4 * MIB),
    )(transmission)

    def exchange(axis, near, far):
        from_far = swapped(far, axis, FAR)
        return swapped(near, axis, NEAR), from_far

    near_outer, far_outer = exchange("narrow", near_outer, far_outer)
    near_columns, far_columns, near_middle, far_middle = pl.pallas_call(
        edges_kernel, name="edges",
        out_shape=[pltpu.VMEM(shape, f32) for shape in (side, side, middle, middle)],
        in_specs=[HBM], out_specs=[VMEM] * 4,
        scratch_shapes=[pltpu.SemaphoreType.DMA((8,))],
        compiler_params=pltpu.CompilerParams(vmem_limit_bytes=4 * MIB),
    )(transmission)
    near_columns, far_columns = exchange("wide", near_columns, far_columns)

    table = jnp.asarray(tables(window))
    extended, total, amplitudes, scale, probe, full, plan = pl.pallas_call(
        setup_kernel, name="setup",
        out_shape=[
            pltpu.VMEM(whole, f32), pltpu.VMEM(whole, f32),
            pltpu.VMEM((2 * slots, 2, window, LANES), f32), pltpu.VMEM((8, LANES), f32),
            pltpu.VMEM(probe_wave.shape, f32),
            pltpu.VMEM((7, *table.shape[1:]), table.dtype),
            jax.ShapeDtypeStruct((HEAD + 6 * slots,), jnp.int32)],
        in_specs=[HBM] * 6, out_specs=[VMEM] * 6 + [SMEM],
        scratch_shapes=[
            pltpu.VMEM(table.shape, table.dtype),
            pltpu.SMEM((1, 1, 2, 2, slots), jnp.int32), pltpu.SMEM(counts.shape, jnp.int32),
            pltpu.SemaphoreType.DMA((4 + 2 * (tiles - 2),)),
            pltpu.SemaphoreType.DMA((2 * slots, 2))],
        compiler_params=pltpu.CompilerParams(vmem_limit_bytes=12 * MIB),
        cost_estimate=pl.CostEstimate(
            flops=0, bytes_accessed=8 * MIB, transcendentals=0),
    )(*(pltpu.with_memory_space_constraint(x, pltpu.HBM)
        for x in (jnp.swapaxes(positions, 3, 4), counts, transmission, measured, probe_wave,
                  table)))
    common = (plan, scale, probe, full, amplitudes)

    def small_kernel(kernel, outs, *ins):
        return pl.pallas_call(
            kernel,
            out_shape=[pltpu.VMEM(shape, f32) for shape in outs],
            in_specs=[VMEM] * len(ins), out_specs=[VMEM] * len(outs),
            compiler_params=pltpu.CompilerParams(vmem_limit_bytes=4 * MIB),
        )(*ins)

    both = (2, 2 * HALO, HALO)
    near_corner, far_corner = exchange(
        "wide", *small_kernel(ends_kernel, [both] * 2, near_outer, far_outer))
    near_middle, far_middle = exchange("narrow", near_middle, far_middle)

    inner_tiles, ends = tuple(range(2, tiles - 2)), (1, tiles - 2)
    beside = (("wide", NEAR),), (("wide", FAR),)

    def rim(which, middle_at, ends_at, corners_at):
        row = ("narrow", which)
        return ((middle_at, 0, row, HALO, inner_tiles), (ends_at, 0, row, HALO, ends),
                *((corners_at + other, which * HALO, row, HALO, beside[other])
                  for other in (NEAR, FAR)))

    def columns_at(first):
        return tuple((first + which, 0, HALO, height, beside[which]) for which in (NEAR, FAR))

    def rim_out(which):
        row = ("narrow", which)
        return ((0, 0, row, HALO, inner_tiles), (1, 0, row, HALO, ends),
                (2, 0, row, HALO, beside[NEAR]), (3, 0, row, HALO, beside[FAR]))

    rims = [middle, outer, small_rim, small_rim]

    def folded(rim_ends, near_rim, far_rim):
        near_rim, far_rim = exchange("wide", near_rim, far_rim)
        out, = small_kernel(folded_kernel, [outer], rim_ends, near_rim, far_rim)
        return out

    extended, total, near_up, near_ends, *corners = run_slots(
        True, common, extended, total,
        (near_middle, near_outer, near_corner, far_corner, near_columns, far_columns),
        rim(NEAR, 0, 1, 2) + columns_at(4), rim_out(NEAR), rims)
    near_ends = folded(near_ends, *corners)
    extended, total, far_up, far_ends, *corners, near_side, far_side = run_slots(
        False, common, extended, total,
        (far_middle, far_outer, near_corner, far_corner), rim(FAR, 0, 1, 2),
        rim_out(FAR) + columns_at(4), rims + [side, side])
    far_ends = folded(far_ends, *corners)
    near_up, far_up = exchange("narrow", near_up, far_up)
    near_ends, far_ends = exchange("narrow", near_ends, far_ends)
    near_side, far_side = exchange("wide", near_side, far_side)

    out, head, foot = pl.pallas_call(
        tail_kernel, name="tail",
        out_shape=[jax.ShapeDtypeStruct((2, height, width), f32),
                   pltpu.VMEM(wide_rim, f32), pltpu.VMEM(wide_rim, f32)],
        in_specs=[VMEM] * 6, out_specs=[ANY, VMEM, VMEM],
        scratch_shapes=[pltpu.VMEM((2, height, width), f32), pltpu.SemaphoreType.DMA((2,))],
        compiler_params=pltpu.CompilerParams(vmem_limit_bytes=8 * MIB),
    )(extended, total, near_side, far_side, near_up, far_up)
    return pl.pallas_call(
        rims_kernel, name="rims",
        out_shape=jax.ShapeDtypeStruct((2, height, width), f32),
        in_specs=[VMEM] * 4 + [ANY], out_specs=ANY,
        input_output_aliases={4: 0},
        scratch_shapes=[pltpu.VMEM(wide_rim, f32), pltpu.VMEM(wide_rim, f32),
                        pltpu.SemaphoreType.DMA((4,))],
        compiler_params=pltpu.CompilerParams(vmem_limit_bytes=4 * MIB),
    )(head, foot, near_ends, far_ends, out)


def solution(mesh):
    in_specs = (
        P(None, "narrow", "wide"),
        P(),
        P("narrow", "wide", None, None, None),
        P("narrow", "wide", None),
        P("narrow", "wide", None, None, None, None),
    )
    out_specs = P(None, "narrow", "wide")
    return jax.shard_map(update, mesh=mesh, in_specs=in_specs, out_specs=out_specs, check_vma=False)
```
